32 devices in a mesh: top: 4 (over x, core), mid: 2 (over y), leaf: 4 (over z).
Axes of the slice: x: 2, y: 2, z: 4, core: 2. Of those that a mesh axis runs over, the one named last changes fastest.
Arguments:
- rhs: bfloat16 [49152, 256], P(('top', 'mid', 'leaf')), may hold values from -6 to 6
- guess: bfloat16 [49152, 256], P(('top', 'mid', 'leaf')), may hold values from -3 to 3
- diag_blocks: bfloat16 [32, 1536, 1536], P(('top', 'mid', 'leaf')), as said below
- precond: bfloat16 [32, 1536, 1536], P(('top', 'mid', 'leaf'))
- bases: bfloat16 [32, 1536, 128], P(('top', 'mid', 'leaf')), may hold values from -0.3125 to 0.3125
- leaf_to_middle_transfer: bfloat16 [32, 128, 128], P(('top', 'mid', 'leaf')), may hold values from -0.25 to 0.25
- mid_transfer: bfloat16 [8, 128, 128], replicated, may hold values from -0.375 to 0.375
- leaf_coupling: bfloat16 [32, 4, 128, 128], P(('top', 'mid', 'leaf')), may hold values from -0.25 to 0.25
- cluster_coupling: bfloat16 [8, 3, 128, 128], P(('top', 'mid')), may hold values from -0.3125 to 0.3125
- group_coupling: bfloat16 [4, 2, 128, 128], P('top'), may hold values from -0.375 to 0.375
- leaf_lists: int32 [32, 4], P(('top', 'mid', 'leaf')), may hold values from 0 to 3, as said below
- owner: int32 [8, 4], P(('top', 'mid')), may hold values from 0 to 3, as said below
- cluster_lists: int32 [8, 3], P(('top', 'mid')), may hold values from 0 to 7, as said below
- group_lists: int32 [4, 2], P('top'), may hold values from 0 to 3, as said below
Outputs:
- solution: bfloat16 [49152, 256], P(('top', 'mid', 'leaf'))
The draws below stay inside these ranges and needn't reach their ends.
Inputs may be any that keep to these rules, and one draw needn't show every extreme that they name: `leaf_lists`: each row holds 4 distinct sibling cluster ids. `owner`: each row is a permutation of the slots of the cluster. `cluster_lists`: each row holds 3 distinct cluster ids. `group_lists`: each row holds 2 distinct group ids. `diag_blocks`: each block is a diagonal with entries from 1 to 3 plus small dense noise.
All inputs are finite; a program needn't handle non-finite values.
Results may differ from the reference program's by a relative error of at most 0.028.
Values may be sent and summed in bfloat16 or wider, within the bound.
No kernel may reach another device: no remote copies, remote signals or barrier semaphores. Data moves between devices by JAX's collectives and lax.ppermute only.
A program may use at most 64 MiB of HBM per device.

```python
import jax
import jax.numpy as jnp
from jax import lax

LEAF_N = 1536
RANK = 128
RHS = 256
K0 = 4
K2 = 3
K1 = 2
NTOP = 4
NMID = 8
LEAF_PER = 4
NLEAF = 32
N = 49152


def draw_diag_blocks(key, part):
    first_key, second_key = jax.random.split(jax.random.fold_in(key, 11))
    diagonal = jnp.exp(jax.random.uniform(first_key, (NLEAF, LEAF_N), jnp.float32, 0.0, 1.0986))
    noise_part = jax.random.normal(second_key, (NLEAF, LEAF_N, LEAF_N), jnp.float32) / jnp.sqrt(LEAF_N * 1.0)
    identity = jnp.eye(LEAF_N, dtype=jnp.float32)
    return (noise_part + diagonal[:, :, None] * identity).astype(jnp.bfloat16)


def draw_precond(key, part):
    first_key, second_key = jax.random.split(jax.random.fold_in(key, 23))
    diagonal = jnp.exp(jax.random.uniform(first_key, (NLEAF, LEAF_N), jnp.float32, -1.386, -0.693))
    noise_part = 0.2 * jax.random.normal(second_key, (NLEAF, LEAF_N, LEAF_N), jnp.float32) / jnp.sqrt(LEAF_N * 1.0)
    identity = jnp.eye(LEAF_N, dtype=jnp.float32)
    return (noise_part + diagonal[:, :, None] * identity).astype(jnp.bfloat16)


def distinct_rows(key, salt, rows, choose, total):
    subkeys = jax.random.split(jax.random.fold_in(key, salt), rows)
    return jax.vmap(lambda single: jax.random.permutation(single, total)[:choose])(subkeys).astype(jnp.int32)


def draw_leaf_lists(key, part):
    return distinct_rows(key, 31, NLEAF, K0, LEAF_PER)


def draw_owner(key, part):
    return distinct_rows(key, 37, NMID, LEAF_PER, LEAF_PER)


def draw_cluster_lists(key, part):
    return distinct_rows(key, 41, NMID, K2, NMID)


def draw_group_lists(key, part):
    return distinct_rows(key, 43, NTOP, K1, NTOP)


def block_scale(stream_key, dims, cuts, least, largest):
    level = 1.0
    for axis_at, blocks in cuts:
        draws = jax.random.uniform(jax.random.fold_in(jax.random.fold_in(stream_key, 6), axis_at), (blocks,), jnp.float32, least / len(cuts), largest / len(cuts))
        level = level * jnp.repeat(jnp.exp(draws), dims[axis_at] // blocks).reshape((-1,) + (1,) * (len(dims) - 1 - axis_at))
    return level


def normal_values(stream_key, dims, deviation, limit, cuts=(), kind=jnp.bfloat16):
    array = jax.random.normal(stream_key, dims, jnp.float32) * deviation
    if len(cuts) > 0:
        array = block_scale(stream_key, dims, cuts, -0.22, 0.18) * array
    return jnp.clip(array, min=-limit, max=limit).astype(kind)


def setup_inputs(seed: int = 0) -> dict:
    splits = jax.random.split(jax.random.key(seed), 15)
    rhs = normal_values(splits[0], (N, RHS), 1.0, 6.0, ((0, 32),))
    guess = normal_values(splits[1], (N, RHS), 0.5, 3.0, ((0, 32),))
    diag_blocks = draw_diag_blocks(jax.random.fold_in(splits[14], 71), 0)
    precond = draw_precond(jax.random.fold_in(splits[14], 71), 0)
    bases = normal_values(splits[4], (NLEAF, LEAF_N, RANK), (LEAF_N // 4) ** -0.5, 0.3125, ((0, 32),))
    leaf_to_middle_transfer = normal_values(splits[5], (NLEAF, RANK, RANK), (4 * RANK) ** -0.5, 0.25, ((0, 32),))
    mid_transfer = normal_values(splits[6], (NMID, RANK, RANK), (2 * RANK) ** -0.5, 0.375)
    leaf_coupling = normal_values(splits[7], (NLEAF, K0, RANK, RANK), (RANK * K0) ** -0.5, 0.25, ((0, 32),))
    cluster_coupling = normal_values(splits[8], (NMID, K2, RANK, RANK), (RANK * K2) ** -0.5, 0.3125, ((0, 8),))
    group_coupling = normal_values(splits[9], (NTOP, K1, RANK, RANK), (RANK * K1) ** -0.5, 0.375, ((0, 4),))
    leaf_lists = draw_leaf_lists(jax.random.fold_in(splits[14], 71), 0)
    owner = draw_owner(jax.random.fold_in(splits[14], 71), 0)
    cluster_lists = draw_cluster_lists(jax.random.fold_in(splits[14], 71), 0)
    group_lists = draw_group_lists(jax.random.fold_in(splits[14], 71), 0)
    return {"rhs": rhs, "guess": guess, "diag_blocks": diag_blocks, "precond": precond, "bases": bases, "leaf_to_middle_transfer": leaf_to_middle_transfer, "mid_transfer": mid_transfer, "leaf_coupling": leaf_coupling, "cluster_coupling": cluster_coupling, "group_coupling": group_coupling, "leaf_lists": leaf_lists, "owner": owner, "cluster_lists": cluster_lists, "group_lists": group_lists}


damping = 0.7


def near_part(diag_blocks, blocks):
    def one_block(pair):
        return jnp.dot(pair[0], pair[1], preferred_element_type=jnp.float32)
    return lax.map(one_block, (diag_blocks, blocks))


def apply_matrix(vector, diag_blocks, bases, leaf_to_middle_transfer, mid_transfer, leaf_coupling, cluster_coupling, group_coupling, leaf_lists, owner, cluster_lists, group_lists):
    single_precision = jnp.float32
    brain_float_sixteen = jnp.bfloat16
    blocks = vector.reshape(NLEAF, LEAF_N, RHS)
    leaf_coefficient = jnp.einsum('sna,snr->sar', bases.astype(single_precision), blocks.astype(single_precision)).astype(brain_float_sixteen)
    upward_contribution = jnp.einsum('euw,euk->ewk', leaf_to_middle_transfer.astype(single_precision), leaf_coefficient.astype(single_precision)).astype(brain_float_sixteen)
    cluster_coef = jnp.sum(upward_contribution.astype(single_precision).reshape(NMID, LEAF_PER, RANK, RHS), axis=1).astype(brain_float_sixteen)
    group_terms = jnp.einsum('cba,cbr->car', mid_transfer.astype(single_precision), cluster_coef.astype(single_precision))
    group_coef = jnp.sum(group_terms.reshape(NTOP, NMID // NTOP, RANK, RHS), axis=1).astype(brain_float_sixteen)
    slots = jnp.take_along_axis(owner, leaf_lists.reshape(NMID, LEAF_PER * K0), axis=1)
    leaf_table = leaf_coefficient.reshape(NMID, LEAF_PER, RANK, RHS)
    picked = jax.vmap(lambda table, index: jnp.take(table, index, axis=0))(leaf_table, slots)
    picked = picked.reshape(NLEAF, K0, RANK, RHS)
    leaf_distant_field = jnp.einsum('skab,skbr->sar', leaf_coupling.astype(single_precision), picked.astype(single_precision))
    cluster_far = jnp.einsum('ckab,ckbr->car', cluster_coupling.astype(single_precision), jnp.take(cluster_coef, cluster_lists, axis=0).astype(single_precision))
    group_far = jnp.einsum('gkab,gkbr->gar', group_coupling.astype(single_precision), jnp.take(group_coef, group_lists, axis=0).astype(single_precision)).astype(brain_float_sixteen)
    group_rep = jnp.repeat(group_far, NMID // NTOP, axis=0)
    cluster_total = (cluster_far + jnp.einsum('cab,cbr->car', mid_transfer.astype(single_precision), group_rep.astype(single_precision))).astype(brain_float_sixteen)
    cluster_representative = jnp.repeat(cluster_total, LEAF_PER, axis=0)
    leaf_grand_total = (leaf_distant_field + jnp.einsum('mwo,mon->mwn', leaf_to_middle_transfer.astype(single_precision), cluster_representative.astype(single_precision))).astype(brain_float_sixteen)
    far_part = jnp.einsum('sna,sar->snr', bases.astype(single_precision), leaf_grand_total.astype(single_precision))
    return (near_part(diag_blocks, blocks) + far_part).reshape(N, RHS)


def reference(rhs, guess, diag_blocks, precond, bases, leaf_to_middle_transfer, mid_transfer, leaf_coupling, cluster_coupling, group_coupling, leaf_lists, owner, cluster_lists, group_lists):
    def apply_a(vector):
        return apply_matrix(vector, diag_blocks, bases, leaf_to_middle_transfer, mid_transfer, leaf_coupling, cluster_coupling, group_coupling, leaf_lists, owner, cluster_lists, group_lists)

    def smooth(residual):
        blocks = residual.astype(jnp.bfloat16).reshape(NLEAF, LEAF_N, RHS)
        return near_part(precond, blocks).reshape(N, RHS)

    residual = rhs.astype(jnp.float32) - apply_a(guess)
    first = guess.astype(jnp.float32) + damping * smooth(residual)
    residual = rhs.astype(jnp.float32) - apply_a(first.astype(jnp.bfloat16))
    second = first + damping * smooth(residual)
    return second.astype(jnp.bfloat16)
```

```python
import functools

import jax
import jax.numpy as jnp
from jax import lax
from jax.experimental import pallas as pl
from jax.experimental.pallas import tpu as pltpu
from jax.sharding import PartitionSpec as P

damping = 0.7
f32 = jnp.float32
bf16 = jnp.bfloat16
VMEM = pl.BlockSpec(memory_space=pltpu.VMEM)
SMEM = pl.BlockSpec(memory_space=pltpu.SMEM)


def mm(a, b):
    return jnp.dot(a, b, preferred_element_type=f32)


def mtm(a, b):
    return lax.dot_general(a, b, (((0,), (0,)), ((), ())), preferred_element_type=f32)


def call(kernel, outs, args, specs, scratch=(), limit=16, name=None, flops=0, nbytes=0):
    return pl.pallas_call(
        kernel,
        out_shape=outs,
        in_specs=specs,
        out_specs=jax.tree.map(lambda _: VMEM, outs),
        scratch_shapes=list(scratch),
        compiler_params=pltpu.CompilerParams(vmem_limit_bytes=limit << 20),
        cost_estimate=pl.CostEstimate(flops=flops, bytes_accessed=nbytes, transcendentals=0),
        name=name,
    )(*args)


def shape(dims, kind):
    return jax.ShapeDtypeStruct(dims, kind)


def power_of_two(n):
    return n & (n - 1) == 0


def exchange(value, axes, size, steps):
    return [lax.ppermute(value, axes, [(i, i ^ step) for i in range(size)]) for step in steps]


def gather_leaf(value, size):
    if power_of_two(size) and size <= 8:
        return [value] + exchange(value, "leaf", size, range(1, size))
    everything = lax.all_gather(value, "leaf")
    here = lax.axis_index("leaf")
    order = (here ^ jnp.arange(size)) if power_of_two(size) else jnp.arange(size)
    everything = jnp.take(everything, order, axis=0)
    return [everything[k] for k in range(size)]


def gather_clusters(value, tops, mids):
    size = tops * mids
    rows = value.shape[0]
    partner = lax.ppermute(value, "top", [(i, i ^ 1) for i in range(tops)])
    both = jnp.concatenate([value, partner])
    steps = [q for q in range(1, size) if not q & mids]
    return [both] + exchange(both, ("top", "mid"), size, steps), [0] + steps


def coef_kernel(bases, guess, out):
    out[...] = mtm(bases[...], guess[...]).astype(bf16)


def near_kernel(tile, guess, rhs, diag, precond, bases, transfer, f0, r7, coef, wmat, w1, f0b):
    rows = guess.shape[0]
    for at in range(0, rows, tile):
        here = pl.ds(at, tile)
        product = mm(diag[here, :], guess[...])
        w1[here, :] = (rhs[here, :].astype(f32) - product).astype(bf16)
    for at in range(0, rows, tile):
        here = pl.ds(at, tile)
        block = precond[here, :]
        first = guess[here, :].astype(f32) + damping * mm(block, w1[...])
        f0[here, :] = first
        f0b[here, :] = first.astype(bf16)
        r7[here, :] = (damping * mm(block, bases[...])).astype(bf16)
    flipped = bases[...].T
    coef[...] = mm(flipped, f0b[...])
    gmat = mm(flipped, r7[...]).astype(bf16)
    wmat[0] = gmat
    wmat[1] = mm(gmat, transfer[...]).astype(bf16)


def leaf_kernel(size, here, slots, coupling, coef, gw, *refs):
    coefs, transfers = refs[:size], refs[size : 2 * size]
    cluster, leaf_far, second, table = refs[2 * size :]
    total = None
    for k in range(size):
        table[here[0] ^ k] = coefs[k][...]
        up = mtm(transfers[k][...], coefs[k][...]).astype(bf16).astype(f32)
        total = up if total is None else total + up
    cluster[...] = total.astype(bf16)
    far = None
    for k in range(coupling.shape[0]):
        term = mm(coupling[k], table[slots[k]])
        far = term if far is None else far + term
    leaf_far[...] = far
    second[...] = (coef[...] - mm(gw[0], far.astype(bf16))).astype(bf16)


def cluster_total(mids, place, cluster_lists, group_lists, mid_transfer, cc, gc, packs, steps, table):
    rank = cc.shape[1]
    for pack, step in zip(packs, steps):
        table[place[1] ^ step] = pack[:rank, :]
        table[place[1] ^ step ^ mids] = pack[rank:, :]
    far = None
    for k in range(gc.shape[0]):
        coef = None
        for m in range(mids):
            at = group_lists[k] * mids + m
            term = mtm(mid_transfer[at], table[at])
            coef = term if coef is None else coef + term
        term = mm(gc[k], coef.astype(bf16))
        far = term if far is None else far + term
    total = mm(mid_transfer[place[1]], far.astype(bf16))
    for k in range(cc.shape[0]):
        total = total + mm(cc[k], table[cluster_lists[k]])
    return total.astype(bf16)


def middle_kernel(size, mids, steps, place, cluster_lists, group_lists, mid_transfer, cc, gc, *refs):
    n = len(steps)
    packs, refs = refs[:n], refs[n:]
    transfers, refs = refs[:size], refs[size:]
    seconds, refs = refs[:size], refs[size:]
    wmats, refs = refs[:size], refs[size:]
    cluster, ctot, coefs, table = refs
    total1 = cluster_total(
        mids, place, cluster_lists, group_lists, mid_transfer, cc, gc, packs, steps, table
    )
    ctot[...] = total1
    total = None
    for k in range(size):
        c2 = (seconds[k][...].astype(f32) - mm(wmats[k][...], total1)).astype(bf16)
        coefs[place[0] ^ k] = c2
        up = mtm(transfers[k][...], c2).astype(bf16).astype(f32)
        total = up if total is None else total + up
    cluster[...] = total.astype(bf16)


def second_kernel(tile, slots, rhs, diag, precond, r7, f0, lf1, ctot, transfer, coupling, coefs, out, lf2, fb, w2):
    rows = rhs.shape[0]
    total = (lf1[...] + mm(transfer[...], ctot[...])).astype(bf16)
    for at in range(0, rows, tile):
        here = pl.ds(at, tile)
        first = f0[here, :] - mm(r7[here, :], total)
        out[here, :] = first
        fb[here, :] = first.astype(bf16)
    far = None
    for k in range(coupling.shape[0]):
        term = mm(coupling[k], coefs[slots[k]])
        far = term if far is None else far + term
    lf2[...] = far
    for at in range(0, rows, tile):
        here = pl.ds(at, tile)
        product = mm(diag[here, :], fb[...])
        w2[here, :] = (rhs[here, :].astype(f32) - product).astype(bf16)
    for at in range(0, rows, tile):
        here = pl.ds(at, tile)
        out[here, :] = out[here, :] + damping * mm(precond[here, :], w2[...])


def last_kernel(mids, steps, place, cluster_lists, group_lists, mid_transfer, cc, gc, lf2, transfer, r7, near, *refs):
    n = len(steps)
    packs, refs = refs[:n], refs[n:]
    out, table = refs
    total2 = cluster_total(
        mids, place, cluster_lists, group_lists, mid_transfer, cc, gc, packs, steps, table
    )
    total = (lf2[...] + mm(transfer[...], total2)).astype(bf16)
    out[...] = (near[...] - mm(r7[...], total)).astype(bf16)


def body(
    rhs, guess, diag_blocks, precond, bases, leaf_to_middle_transfer, mid_transfer,
    leaf_coupling, cluster_coupling, group_coupling, leaf_lists, owner, cluster_lists, group_lists,
    *, tops, mids, leaves,
):
    rows, columns = rhs.shape
    rank = bases.shape[2]
    diag, prec, basis = diag_blocks[0], precond[0], bases[0]
    transfer, coupling = leaf_to_middle_transfer[0], leaf_coupling[0]
    cc, gc = cluster_coupling[0], group_coupling[0]
    clists, glists = cluster_lists[0], group_lists[0]
    where = jnp.arange(leaf_lists.shape[1])
    chosen = leaf_lists[0][:, None] == jnp.arange(owner.shape[1])[None, :]
    slots = jnp.sum(jnp.where(chosen, owner[0][None, :], 0), axis=1).astype(jnp.int32)
    leaf_at = lax.axis_index("leaf").astype(jnp.int32)
    cluster_at = lax.axis_index(("top", "mid")).astype(jnp.int32)
    place = jnp.stack([leaf_at, cluster_at])
    tile = rows // 2 if rows % 32 == 0 else rows
    clusters = tops * mids

    transfers = gather_leaf(transfer, leaves)
    coef1 = call(
        coef_kernel, shape((rank, columns), bf16), [basis, guess], [VMEM] * 2, name="coef",
        flops=2 * rows * rank * columns, nbytes=2 * rows * (rank + columns), limit=8,
    )
    coefs1 = gather_leaf(coef1, leaves)
    f0, r7, coef0, gw = call(
        functools.partial(near_kernel, tile),
        (shape((rows, columns), f32), shape((rows, rank), bf16), shape((rank, columns), f32),
         shape((2, rank, rank), bf16)),
        [guess, rhs, diag, prec, basis, transfer], [VMEM] * 6,
        [pltpu.VMEM((rows, columns), bf16)] * 2, name="near", limit=28,
        flops=4 * rows * rows * (columns + rank // 2), nbytes=4 * rows * rows,
    )
    cluster1, lf1, second = call(
        functools.partial(leaf_kernel, leaves),
        (shape((rank, columns), bf16), shape((rank, columns), f32), shape((rank, columns), bf16)),
        [place, slots, coupling, coef0, gw, *coefs1, *transfers],
        [SMEM] * 2 + [VMEM] * (3 + 2 * leaves),
        [pltpu.VMEM((leaves, rank, columns), bf16)], name="leaf",
        flops=2 * rank * rank * columns * (2 * leaves + 1), nbytes=2 * leaves * rank * (columns + rank),
    )
    packs1, steps = gather_clusters(cluster1, tops, mids)
    message = jnp.concatenate([second, gw[1]], axis=1)
    messages = gather_leaf(message, leaves)
    seconds = [m[:, :columns] for m in messages]
    wmats = [m[:, columns:] for m in messages]
    n = len(steps)
    cluster2, ctot, coefs2 = call(
        functools.partial(middle_kernel, leaves, mids, steps),
        (shape((rank, columns), bf16), shape((rank, columns), bf16), shape((leaves, rank, columns), bf16)),
        [place, clists, glists, mid_transfer, cc, gc, *packs1, *transfers, *seconds, *wmats],
        [SMEM] * 3 + [VMEM] * (3 + n + 3 * leaves),
        [pltpu.VMEM((clusters, rank, columns), bf16)], name="middle",
        flops=2 * rank * rank * columns * (2 * leaves + 10), nbytes=2 * leaves * rank * columns,
    )
    packs2, steps = gather_clusters(cluster2, tops, mids)
    near, lf2 = call(
        functools.partial(second_kernel, tile),
        (shape((rows, columns), f32), shape((rank, columns), f32)),
        [slots, rhs, diag, prec, r7, f0, lf1, ctot, transfer, coupling, coefs2],
        [SMEM] + [VMEM] * 10,
        [pltpu.VMEM((rows, columns), bf16)] * 2, name="second", limit=28,
        flops=4 * rows * rows * columns, nbytes=4 * rows * rows,
    )
    return call(
        functools.partial(last_kernel, mids, steps), shape((rows, columns), bf16),
        [place, clists, glists, mid_transfer, cc, gc, lf2, transfer, r7, near, *packs2],
        [SMEM] * 3 + [VMEM] * (7 + n),
        [pltpu.VMEM((clusters, rank, columns), bf16)], name="last",
        flops=2 * rows * rank * columns, nbytes=6 * rows * columns,
    )


def solution(mesh):
    everywhere = ("top", "mid", "leaf")
    in_specs = (
        P(everywhere, None), P(everywhere, None), P(everywhere, None, None), P(everywhere, None, None),
        P(everywhere, None, None), P(everywhere, None, None), P(), P(everywhere, None, None, None),
        P(("top", "mid"), None, None, None), P("top", None, None, None), P(everywhere, None),
        P(("top", "mid"), None), P(("top", "mid"), None), P("top", None),
    )
    run = functools.partial(
        body, tops=mesh.shape["top"], mids=mesh.shape["mid"], leaves=mesh.shape["leaf"]
    )
    return jax.shard_map(
        run, mesh=mesh, in_specs=in_specs, out_specs=P(everywhere, None), check_vma=False
    )
```

```python
import functools

import jax
import jax.numpy as jnp
from jax import lax
from jax.experimental import pallas as pl
from jax.experimental.pallas import tpu as pltpu
from jax.sharding import PartitionSpec as P

damping = 0.7
f32 = jnp.float32
bf16 = jnp.bfloat16
VMEM = pl.BlockSpec(memory_space=pltpu.VMEM)
SMEM = pl.BlockSpec(memory_space=pltpu.SMEM)


def mm(a, b):
    return jnp.dot(a, b, preferred_element_type=f32)


def mtm(a, b):
    return lax.dot_general(a, b, (((0,), (0,)), ((), ())), preferred_element_type=f32)


HBM = pl.BlockSpec(memory_space=pltpu.HBM)


def call(kernel, outs, args, specs, scratch=(), limit=16, name=None, flops=0, nbytes=0, out_spec=VMEM):
    return pl.pallas_call(
        kernel,
        out_shape=outs,
        in_specs=specs,
        out_specs=jax.tree.map(lambda _: out_spec, outs),
        scratch_shapes=list(scratch),
        compiler_params=pltpu.CompilerParams(vmem_limit_bytes=limit << 20),
        cost_estimate=pl.CostEstimate(flops=flops, bytes_accessed=nbytes, transcendentals=0),
        name=name,
    )(*args)


def shape(dims, kind):
    return jax.ShapeDtypeStruct(dims, kind)


def at_home(value):
    return pltpu.with_memory_space_constraint(value, pltpu.HBM)


def spans(rows, parts):
    if rows % (16 * parts):
        parts = 1
    return [pl.ds(k * (rows // parts), rows // parts) for k in range(parts)]


def power_of_two(n):
    return n & (n - 1) == 0


def exchange(value, axes, size, steps):
    return [lax.ppermute(value, axes, [(i, i ^ step) for i in range(size)]) for step in steps]


def gather_leaf(value, size):
    if power_of_two(size) and size <= 8:
        far = exchange(value, "leaf", size, range(size - 1, 0, -1))
        return [value] + far[::-1]
    everything = lax.all_gather(value, "leaf")
    here = lax.axis_index("leaf")
    everything = jnp.take(everything, here ^ jnp.arange(size), axis=0)
    return [everything[k] for k in range(size)]


def gather_clusters(value, tops, mids):
    size = tops * mids
    partner = lax.ppermute(value, "top", [(i, i ^ 1) for i in range(tops)])
    both = jnp.concatenate([value, partner])
    steps = [q for q in range(size - 1, 0, -1) if not q & mids]
    return [both] + exchange(both, ("top", "mid"), size, steps), [0] + steps


def coef_kernel(parts, bases, guess, transfer, message, bases_on, guess_on, transfer_on, sems, sem):
    columns = guess.shape[1]
    cuts = spans(guess.shape[0], parts)
    copies = []
    small = pltpu.make_async_copy(transfer, transfer_on, sem)
    small.start()
    for k, cut in enumerate(cuts):
        first = pltpu.make_async_copy(bases.at[cut, :], bases_on.at[cut, :], sems.at[0, k])
        second = pltpu.make_async_copy(guess.at[cut, :], guess_on.at[cut, :], sems.at[1, k])
        first.start()
        second.start()
        copies.append((first, second))
    small.wait()
    message[:, columns:] = transfer_on[...].T
    total = None
    for cut, (first, second) in zip(cuts, copies):
        first.wait()
        second.wait()
        term = mtm(bases_on[cut, :], guess_on[cut, :])
        total = term if total is None else total + term
    message[:, :columns] = total.astype(bf16)


def near_kernel(
    parts, mids, guess, bases, transfer, groups, middles, group_matrices, rhs, diag, precond,
    diag_on, precond_on, rhs_on, f0, r7, coef, gw, gx, w1, f0b, glists, mid_transfer, gc, sems, small_sems,
):
    cuts = spans(guess.shape[0], parts)

    def fetch(source, target, row):
        copies = []
        for k, cut in enumerate(cuts):
            copy = pltpu.make_async_copy(source.at[cut, :], target.at[cut, :], sems.at[row, k])
            copy.start()
            copies.append(copy)
        return copies

    rhs_copies = fetch(rhs, rhs_on, 0)
    diag_copies = fetch(diag, diag_on, 1)
    small_copies = []
    for k, pair in enumerate(((groups, glists), (middles, mid_transfer), (group_matrices, gc))):
        small_copies.append(pltpu.make_async_copy(*pair, small_sems.at[k]))
        small_copies[-1].start()
    precond_copies = fetch(precond, precond_on, 2)
    flipped = bases[...].T
    for k, cut in enumerate(cuts):
        diag_copies[k].wait()
        rhs_copies[k].wait()
        product = mm(diag_on[cut, :], guess[...])
        w1[cut, :] = (rhs_on[cut, :].astype(f32) - product).astype(bf16)
    for copy in small_copies:
        copy.wait()
    here = lax.axis_index("top") * mids + lax.axis_index("mid")
    for k in range(gc.shape[0]):
        left = mm(mid_transfer[here], gc[k]).astype(bf16)
        for m in range(mids):
            right = mid_transfer[glists[0, k] * mids + m]
            both = lax.dot_general(left, right, (((1,), (1,)), ((), ())), preferred_element_type=f32)
            gx[k * mids + m] = both.astype(bf16)
    for k, cut in enumerate(cuts):
        precond_copies[k].wait()
        block = precond_on[cut, :]
        first = guess[cut, :].astype(f32) + damping * mm(block, w1[...])
        f0[cut, :] = first
        f0b[cut, :] = first.astype(bf16)
        r7[cut, :] = (damping * mm(block, bases[...])).astype(bf16)
    coef[...] = mm(flipped, f0b[...])
    gmat = mm(flipped, r7[...]).astype(bf16)
    gw[0] = gmat
    gw[1] = mm(gmat, transfer[...]).astype(bf16)


def leaf_kernel(size, lists, owner, coupling, coef, gw, *refs):
    messages = refs[:size]
    cluster, leaf_far, message, table = refs[size:]
    rank, columns = coef.shape
    here = lax.axis_index("leaf")
    total = None
    for k in range(size):
        coefs = messages[k][:, :columns]
        table[here ^ k] = coefs
        up = mm(messages[k][:, columns:], coefs).astype(bf16).astype(f32)
        total = up if total is None else total + up
    cluster[...] = total.astype(bf16)
    far = None
    for k in range(coupling.shape[0]):
        term = mm(coupling[k], table[owner[0, lists[0, k]]])
        far = term if far is None else far + term
    leaf_far[...] = far
    message[:, :columns] = (coef[...] - mm(gw[0], far.astype(bf16))).astype(bf16)
    message[:, columns:] = gw[1]


def fold_kernel(size, *refs):
    first, second = refs[:size], refs[size : 2 * size]
    base, hmat = refs[2 * size :]
    columns = base.shape[1]
    total = None
    for k in range(size):
        term = mm(first[k][:, columns:], second[k][...])
        total = term if total is None else total + term
    base[...] = total[:, :columns]
    hmat[...] = total[:, columns:].astype(bf16)


def cluster_total(mids, clists, glists, cc, gx, packs, steps, table):
    rank = cc.shape[1]
    here = lax.axis_index("top") * mids + lax.axis_index("mid")
    for pack, step in zip(packs, steps):
        table[here ^ step] = pack[:rank, :]
        table[here ^ step ^ mids] = pack[rank:, :]
    total = None
    for k in range(cc.shape[0]):
        term = mm(cc[k], table[clists[0, k]])
        total = term if total is None else total + term
    for k in range(gx.shape[0] // mids):
        for m in range(mids):
            total = total + mm(gx[k * mids + m], table[glists[0, k] * mids + m])
    return total.astype(bf16)


def middle_kernel(mids, steps, clists, glists, cc, gx, base, hmat, *refs):
    packs = refs[: len(steps)]
    cluster, ctot, table = refs[len(steps) :]
    total = cluster_total(mids, clists, glists, cc, gx, packs, steps, table)
    ctot[...] = total
    cluster[...] = (base[...] - mm(hmat[...], total)).astype(bf16)


def second_kernel(parts, size, lists, owner, rhs, diag, precond, r7, f0, lf1, ctot, transfer, coupling, *refs):
    messages = refs[:size]
    out, lf2, fb, w2, table = refs[size:]
    columns = ctot.shape[1]
    cuts = spans(rhs.shape[0], parts)
    total = (lf1[...] + mm(transfer[...], ctot[...])).astype(bf16)
    for cut in cuts:
        first = f0[cut, :] - mm(r7[cut, :], total)
        out[cut, :] = first
        fb[cut, :] = first.astype(bf16)
    for cut in cuts:
        product = mm(diag[cut, :], fb[...])
        w2[cut, :] = (rhs[cut, :].astype(f32) - product).astype(bf16)
    for cut in cuts:
        out[cut, :] = out[cut, :] + damping * mm(precond[cut, :], w2[...])
    here = lax.axis_index("leaf")
    for k in range(size):
        change = mm(messages[k][:, columns:], ctot[...])
        table[here ^ k] = (messages[k][:, :columns].astype(f32) - change).astype(bf16)
    far = None
    for k in range(coupling.shape[0]):
        term = mm(coupling[k], table[owner[0, lists[0, k]]])
        far = term if far is None else far + term
    lf2[...] = far


def last_kernel(parts, mids, steps, clists, glists, cc, gx, lf2, transfer, r7, near, *refs):
    packs = refs[: len(steps)]
    out, table, result, sems = refs[len(steps) :]
    total2 = cluster_total(mids, clists, glists, cc, gx, packs, steps, table)
    total = (lf2[...] + mm(transfer[...], total2)).astype(bf16)
    copies = []
    for k, cut in enumerate(spans(near.shape[0], parts)):
        result[cut, :] = (near[cut, :] - mm(r7[cut, :], total)).astype(bf16)
        copy = pltpu.make_async_copy(result.at[cut, :], out.at[cut, :], sems.at[k])
        copy.start()
        copies.append(copy)
    for copy in copies:
        copy.wait()


def body(
    rhs, guess, diag_blocks, precond, bases, leaf_to_middle_transfer, mid_transfer,
    leaf_coupling, cluster_coupling, group_coupling, leaf_lists, owner, cluster_lists, group_lists,
    *, tops, mids, leaves,
):
    rows, columns = rhs.shape
    rank = bases.shape[2]
    diag, prec, basis = diag_blocks[0], precond[0], bases[0]
    transfer, coupling = leaf_to_middle_transfer[0], leaf_coupling[0]
    cc, gc = cluster_coupling[0], group_coupling[0]
    clusters = tops * mids
    parts = 3
    dma = pltpu.SemaphoreType.DMA
    coef_bytes = rank * columns * 2

    message1, basis_on, guess_on, transfer_on = call(
        functools.partial(coef_kernel, parts),
        (shape((rank, columns + rank), bf16), shape((rows, rank), bf16), shape((rows, columns), bf16),
         shape((rank, rank), bf16)),
        [at_home(basis), at_home(guess), at_home(transfer)], [HBM] * 3, [dma((2, parts)), dma(())], name="coef",
        flops=2 * rows * rank * columns, nbytes=2 * rows * (rank + columns), limit=8,
    )
    messages1 = gather_leaf(message1, leaves)
    diag_on, prec_on, rhs_on, f0, r7, coef0, gw, gx = call(
        functools.partial(near_kernel, parts, mids),
        (shape((rows, rows), bf16), shape((rows, rows), bf16), shape((rows, columns), bf16),
         shape((rows, columns), f32), shape((rows, rank), bf16), shape((rank, columns), f32),
         shape((2, rank, rank), bf16), shape((gc.shape[0] * mids, rank, rank), bf16)),
        [guess_on, basis_on, transfer_on]
        + [at_home(value) for value in (group_lists, mid_transfer, gc, rhs, diag, prec)],
        [VMEM] * 3 + [HBM] * 6,
        [pltpu.VMEM((rows, columns), bf16)] * 2
        + [pltpu.SMEM(group_lists.shape, jnp.int32), pltpu.VMEM(mid_transfer.shape, bf16), pltpu.VMEM(gc.shape, bf16)]
        + [dma((3, parts)), dma((3,))], name="near", limit=24,
        flops=4 * rows * rows * (columns + rank // 2), nbytes=4 * rows * rows,
    )
    cluster1, lf1, message2 = call(
        functools.partial(leaf_kernel, leaves),
        (shape((rank, columns), bf16), shape((rank, columns), f32), shape((rank, columns + rank), bf16)),
        [leaf_lists, owner, coupling, coef0, gw, *messages1],
        [SMEM] * 2 + [VMEM] * (3 + leaves),
        [pltpu.VMEM((leaves, rank, columns), bf16)], name="leaf",
        flops=2 * rank * rank * columns * (2 * leaves + 1), nbytes=2 * leaves * coef_bytes,
    )
    packs1, steps = gather_clusters(cluster1, tops, mids)
    messages2 = gather_leaf(message2, leaves)
    n = len(steps)
    base, hmat = call(
        functools.partial(fold_kernel, leaves),
        (shape((rank, columns), f32), shape((rank, rank), bf16)),
        [*messages1, *messages2], [VMEM] * (2 * leaves), name="fold",
        flops=2 * rank * rank * columns * 2 * leaves, nbytes=3 * leaves * coef_bytes,
    )
    cluster2, ctot = call(
        functools.partial(middle_kernel, mids, steps),
        (shape((rank, columns), bf16), shape((rank, columns), bf16)),
        [cluster_lists, group_lists, cc, gx, base, hmat, *packs1],
        [SMEM] * 2 + [VMEM] * (4 + n),
        [pltpu.VMEM((clusters, rank, columns), bf16)], name="middle",
        flops=2 * rank * rank * columns * 10, nbytes=2 * clusters * coef_bytes,
    )
    packs2, steps = gather_clusters(cluster2, tops, mids)
    near, lf2 = call(
        functools.partial(second_kernel, parts, leaves),
        (shape((rows, columns), f32), shape((rank, columns), f32)),
        [leaf_lists, owner, rhs_on, diag_on, prec_on, r7, f0, lf1, ctot, transfer_on, coupling, *messages2],
        [SMEM] * 2 + [VMEM] * (9 + leaves),
        [pltpu.VMEM((rows, columns), bf16)] * 2 + [pltpu.VMEM((leaves, rank, columns), bf16)],
        name="second", limit=24,
        flops=4 * rows * rows * columns, nbytes=4 * rows * rows,
    )
    return call(
        functools.partial(last_kernel, parts, mids, steps), shape((rows, columns), bf16),
        [cluster_lists, group_lists, cc, gx, lf2, transfer_on, r7, near, *packs2],
        [SMEM] * 2 + [VMEM] * (6 + n),
        [pltpu.VMEM((clusters, rank, columns), bf16), pltpu.VMEM((rows, columns), bf16), dma((parts,))],
        name="last", out_spec=HBM,
        flops=2 * rows * rank * columns, nbytes=6 * rows * columns,
    )


def solution(mesh):
    everywhere = ("top", "mid", "leaf")
    in_specs = (
        P(everywhere, None), P(everywhere, None), P(everywhere, None, None), P(everywhere, None, None),
        P(everywhere, None, None), P(everywhere, None, None), P(), P(everywhere, None, None, None),
        P(("top", "mid"), None, None, None), P("top", None, None, None), P(everywhere, None),
        P(("top", "mid"), None), P(("top", "mid"), None), P("top", None),
    )
    run = functools.partial(
        body, tops=mesh.shape["top"], mids=mesh.shape["mid"], leaves=mesh.shape["leaf"]
    )
    return jax.shard_map(
        run, mesh=mesh, in_specs=in_specs, out_specs=P(everywhere, None), check_vma=False
    )
```

```python
import functools

import jax
import jax.numpy as jnp
from jax import lax
from jax.experimental import pallas as pl
from jax.experimental.pallas import tpu as pltpu
from jax.sharding import PartitionSpec as P


damping = 0.7
f32 = jnp.float32
bf16 = jnp.bfloat16
VMEM = pl.BlockSpec(memory_space=pltpu.VMEM)
SMEM = pl.BlockSpec(memory_space=pltpu.SMEM)


def mm(a, b):
    return jnp.dot(a, b, preferred_element_type=f32)


def mtm(a, b):
    return lax.dot_general(a, b, (((0,), (0,)), ((), ())), preferred_element_type=f32)


HBM = pl.BlockSpec(memory_space=pltpu.HBM)


def call(kernel, outs, args, specs, scratch=(), limit=16, flops=0, nbytes=0, out_spec=VMEM):
    return pl.pallas_call(
        kernel,
        out_shape=outs,
        in_specs=specs,
        out_specs=jax.tree.map(lambda _: out_spec, outs),
        scratch_shapes=list(scratch),
        compiler_params=pltpu.CompilerParams(vmem_limit_bytes=limit << 20),
        cost_estimate=pl.CostEstimate(flops=flops, bytes_accessed=nbytes, transcendentals=0),
    )(*args)


def shape(dims, kind):
    return jax.ShapeDtypeStruct(dims, kind)


def at_home(value):
    return pltpu.with_memory_space_constraint(value, pltpu.HBM)


def spans(rows, parts):
    if rows % (16 * parts):
        parts = 1
    return [pl.ds(k * (rows // parts), rows // parts) for k in range(parts)]


def power_of_two(n):
    return n & (n - 1) == 0


def exchange(value, axes, size, steps):
    result = []
    for step in steps:
        result.append(lax.ppermute(value, axes, [(i, i ^ step) for i in range(size)]))
    return result


def gather_leaf(value, size):
    if power_of_two(size) and size <= 8:
        return [value] + exchange(value, "leaf", size, range(1, size))
    everything = lax.all_gather(value, "leaf")
    here = lax.axis_index("leaf")
    everything = jnp.take(everything, here ^ jnp.arange(size), axis=0)
    return [everything[k] for k in range(size)]


def cluster_steps(tops, mids):
    return [q for q in range(tops * mids) if not q & mids]


def gather_clusters(value, tops, mids):
    steps = cluster_steps(tops, mids)[1:]
    stack = jnp.concatenate([value] + exchange(value, ("top", "mid"), tops * mids, steps))
    return [stack, lax.ppermute(stack, "top", [(i, i ^ 1) for i in range(tops)])]


def coef_kernel(parts, bases, guess, transfer, message, bases_on, guess_on, transfer_on, sems, sem):
    columns = guess.shape[1]
    cuts = spans(guess.shape[0], parts)
    copies = []
    small = pltpu.make_async_copy(transfer, transfer_on, sem)
    small.start()
    for k, cut in enumerate(cuts):
        first = pltpu.make_async_copy(bases.at[cut, :], bases_on.at[cut, :], sems.at[0, k])
        second = pltpu.make_async_copy(guess.at[cut, :], guess_on.at[cut, :], sems.at[1, k])
        first.start()
        second.start()
        copies.append((first, second))
    small.wait()
    message[:, columns:] = transfer_on[...].T
    total = None
    for cut, (first, second) in zip(cuts, copies):
        first.wait()
        second.wait()
        term = mtm(bases_on[cut, :], guess_on[cut, :])
        total = term if total is None else total + term
    message[:, :columns] = total.astype(bf16)


def near_kernel(
    parts, mids, guess, bases, transfer, groups, middles, group_matrices, rhs, diag, precond,
    diag_on, precond_on, rhs_on, f0, r7, coef, gw, gx, w1, f0b, glists, mid_transfer, gc, sems, small_sems,
):
    cuts = spans(guess.shape[0], parts)

    def fetch(source, target, row):
        copies = []
        for k, cut in enumerate(cuts):
            copy = pltpu.make_async_copy(source.at[cut, :], target.at[cut, :], sems.at[row, k])
            copy.start()
            copies.append(copy)
        return copies

    rhs_copies = fetch(rhs, rhs_on, 0)
    diag_copies = fetch(diag, diag_on, 1)
    small_copies = []
    for k, pair in enumerate(((groups, glists), (middles, mid_transfer), (group_matrices, gc))):
        small_copies.append(pltpu.make_async_copy(*pair, small_sems.at[k]))
        small_copies[-1].start()
    precond_copies = fetch(precond, precond_on, 2)
    flipped = bases[...].T
    for k, cut in enumerate(cuts):
        diag_copies[k].wait()
        rhs_copies[k].wait()
        product = mm(diag_on[cut, :], guess[...])
        w1[cut, :] = (rhs_on[cut, :].astype(f32) - product).astype(bf16)
    for copy in small_copies:
        copy.wait()
    here = lax.axis_index("top") * mids + lax.axis_index("mid")
    for k in range(gc.shape[0]):
        left = mm(mid_transfer[here], gc[k]).astype(bf16)
        for m in range(mids):
            right = mid_transfer[glists[0, k] * mids + m]
            both = lax.dot_general(left, right, (((1,), (1,)), ((), ())), preferred_element_type=f32)
            gx[k * mids + m] = both.astype(bf16)
    for k, cut in enumerate(cuts):
        precond_copies[k].wait()
        block = precond_on[cut, :]
        first = guess[cut, :].astype(f32) + damping * mm(block, w1[...])
        f0[cut, :] = first
        f0b[cut, :] = first.astype(bf16)
        r7[cut, :] = (damping * mm(block, bases[...])).astype(bf16)
    coef[...] = mm(flipped, f0b[...])
    gmat = mm(flipped, r7[...]).astype(bf16)
    gw[0] = gmat
    gw[1] = mm(gmat, transfer[...]).astype(bf16)


def leaf_kernel(size, lists, owner, coupling, coef, gw, *refs):
    messages = refs[:size]
    cluster, leaf_far, message, table = refs[size:]
    _, columns = coef.shape
    here = lax.axis_index("leaf")
    total = None
    for k in range(size):
        coefs = messages[k][:, :columns]
        table[here ^ k] = coefs
        up = mm(messages[k][:, columns:], coefs).astype(bf16).astype(f32)
        total = up if total is None else total + up
    cluster[...] = total.astype(bf16)
    far = None
    for k in range(coupling.shape[0]):
        term = mm(coupling[k], table[owner[0, lists[0, k]]])
        far = term if far is None else far + term
    leaf_far[...] = far
    message[:, :columns] = (coef[...] - mm(gw[0], far.astype(bf16))).astype(bf16)
    message[:, columns:] = gw[1]


def fold_kernel(size, *refs):
    first, second = refs[:size], refs[size : 2 * size]
    base, hmat = refs[2 * size :]
    columns = base.shape[1]
    total = None
    for k in range(size):
        term = mm(first[k][:, columns:], second[k][...])
        total = term if total is None else total + term
    base[...] = total[:, :columns]
    hmat[...] = total[:, columns:].astype(bf16)


def cluster_total(mids, clists, glists, cc, gx, packs, steps, table):
    rank = cc.shape[1]
    here = lax.axis_index("top") * mids + lax.axis_index("mid")
    for k, step in enumerate(steps):
        table[here ^ step] = packs[0][k * rank : (k + 1) * rank, :]
        table[here ^ step ^ mids] = packs[1][k * rank : (k + 1) * rank, :]
    total = None
    for k in range(cc.shape[0]):
        term = mm(cc[k], table[clists[0, k]])
        total = term if total is None else total + term
    for k in range(gx.shape[0] // mids):
        for m in range(mids):
            total = total + mm(gx[k * mids + m], table[glists[0, k] * mids + m])
    return total.astype(bf16)


def middle_kernel(mids, steps, clists, glists, cc, gx, base, hmat, *refs):
    packs = refs[:2]
    cluster, ctot, table = refs[2:]
    total = cluster_total(mids, clists, glists, cc, gx, packs, steps, table)
    ctot[...] = total
    cluster[...] = (base[...] - mm(hmat[...], total)).astype(bf16)


def second_kernel(parts, rhs, diag, precond, r7, f0, lf1, ctot, transfer, out, fb, w2):
    cuts = spans(rhs.shape[0], parts)
    total = (lf1[...] + mm(transfer[...], ctot[...])).astype(bf16)
    for cut in cuts:
        first = f0[cut, :] - mm(r7[cut, :], total)
        out[cut, :] = first
        fb[cut, :] = first.astype(bf16)
    for cut in cuts:
        product = mm(diag[cut, :], fb[...])
        w2[cut, :] = (rhs[cut, :].astype(f32) - product).astype(bf16)
    for cut in cuts:
        out[cut, :] = out[cut, :] + damping * mm(precond[cut, :], w2[...])


def sibling_kernel(size, lists, owner, ctot, coupling, *refs):
    messages = refs[:size]
    far_out, table = refs[size:]
    columns = ctot.shape[1]
    here = lax.axis_index("leaf")
    for k in range(size):
        change = mm(messages[k][:, columns:], ctot[...])
        table[here ^ k] = (messages[k][:, :columns].astype(f32) - change).astype(bf16)
    far = None
    for k in range(coupling.shape[0]):
        term = mm(coupling[k], table[owner[0, lists[0, k]]])
        far = term if far is None else far + term
    far_out[...] = far


def last_kernel(parts, mids, steps, clists, glists, cc, gx, lf2, transfer, r7, near, *refs):
    packs = refs[:2]
    out, table, result, sems = refs[2:]
    total2 = cluster_total(mids, clists, glists, cc, gx, packs, steps, table)
    total = (lf2[...] + mm(transfer[...], total2)).astype(bf16)
    copies = []
    for k, cut in enumerate(spans(near.shape[0], parts)):
        result[cut, :] = (near[cut, :] - mm(r7[cut, :], total)).astype(bf16)
        copy = pltpu.make_async_copy(result.at[cut, :], out.at[cut, :], sems.at[k])
        copy.start()
        copies.append(copy)
    for copy in copies:
        copy.wait()


def body(
    rhs, guess, diag_blocks, precond, bases, leaf_to_middle_transfer, mid_transfer,
    leaf_coupling, cluster_coupling, group_coupling, leaf_lists, owner, cluster_lists, group_lists,
    *, tops, mids, leaves,
):
    rows, columns = rhs.shape
    rank = bases.shape[2]
    diag, prec, basis = diag_blocks[0], precond[0], bases[0]
    transfer, coupling = leaf_to_middle_transfer[0], leaf_coupling[0]
    cc, gc = cluster_coupling[0], group_coupling[0]
    clusters = tops * mids
    parts = 3
    dma = pltpu.SemaphoreType.DMA
    coef_bytes = rank * columns * 2

    message1, basis_on, guess_on, transfer_on = call(
        functools.partial(coef_kernel, parts),
        (shape((rank, columns + rank), bf16), shape((rows, rank), bf16), shape((rows, columns), bf16),
         shape((rank, rank), bf16)),
        [at_home(basis), at_home(guess), at_home(transfer)], [HBM] * 3, [dma((2, parts)), dma(())],
        flops=2 * rows * rank * columns, nbytes=2 * rows * (rank + columns), limit=8,
    )
    messages1 = gather_leaf(message1, leaves)
    diag_on, prec_on, rhs_on, f0, r7, coef0, gw, gx = call(
        functools.partial(near_kernel, parts, mids),
        (shape((rows, rows), bf16), shape((rows, rows), bf16), shape((rows, columns), bf16),
         shape((rows, columns), f32), shape((rows, rank), bf16), shape((rank, columns), f32),
         shape((2, rank, rank), bf16), shape((gc.shape[0] * mids, rank, rank), bf16)),
        [guess_on, basis_on, transfer_on]
        + [at_home(value) for value in (group_lists, mid_transfer, gc, rhs, diag, prec)],
        [VMEM] * 3 + [HBM] * 6,
        [pltpu.VMEM((rows, columns), bf16)] * 2
        + [pltpu.SMEM(group_lists.shape, jnp.int32), pltpu.VMEM(mid_transfer.shape, bf16), pltpu.VMEM(gc.shape, bf16)]
        + [dma((3, parts)), dma((3,))], limit=24,
        flops=4 * rows * rows * (columns + rank // 2), nbytes=4 * rows * rows,
    )
    cluster1, lf1, message2 = call(
        functools.partial(leaf_kernel, leaves),
        (shape((rank, columns), bf16), shape((rank, columns), f32), shape((rank, columns + rank), bf16)),
        [leaf_lists, owner, coupling, coef0, gw, *messages1],
        [SMEM] * 2 + [VMEM] * (3 + leaves),
        [pltpu.VMEM((leaves, rank, columns), bf16)],
        flops=2 * rank * rank * columns * (2 * leaves + 1), nbytes=2 * leaves * coef_bytes,
    )
    packs1 = gather_clusters(cluster1, tops, mids)
    messages2 = gather_leaf(message2, leaves)
    steps = cluster_steps(tops, mids)
    base, hmat = call(
        functools.partial(fold_kernel, leaves),
        (shape((rank, columns), f32), shape((rank, rank), bf16)),
        [*messages1, *messages2], [VMEM] * (2 * leaves),
        flops=2 * rank * rank * columns * 2 * leaves, nbytes=3 * leaves * coef_bytes,
    )
    cluster2, ctot = call(
        functools.partial(middle_kernel, mids, steps),
        (shape((rank, columns), bf16), shape((rank, columns), bf16)),
        [cluster_lists, group_lists, cc, gx, base, hmat, *packs1],
        [SMEM] * 2 + [VMEM] * 6,
        [pltpu.VMEM((clusters, rank, columns), bf16)],
        flops=2 * rank * rank * columns * 10, nbytes=2 * clusters * coef_bytes,
    )
    packs2 = gather_clusters(cluster2, tops, mids)
    near = call(
        functools.partial(second_kernel, parts), shape((rows, columns), f32),
        [rhs_on, diag_on, prec_on, r7, f0, lf1, ctot, transfer_on], [VMEM] * 8,
        [pltpu.VMEM((rows, columns), bf16)] * 2, limit=24,
        flops=4 * rows * rows * columns, nbytes=4 * rows * rows,
    )
    lf2 = call(
        functools.partial(sibling_kernel, leaves), shape((rank, columns), f32),
        [leaf_lists, owner, ctot, coupling, *messages2],
        [SMEM] * 2 + [VMEM] * (2 + leaves), [pltpu.VMEM((leaves, rank, columns), bf16)],
        flops=2 * rank * rank * columns * 2 * leaves, nbytes=2 * leaves * coef_bytes,
    )
    return call(
        functools.partial(last_kernel, parts, mids, steps), shape((rows, columns), bf16),
        [cluster_lists, group_lists, cc, gx, lf2, transfer_on, r7, near, *packs2],
        [SMEM] * 2 + [VMEM] * 8,
        [pltpu.VMEM((clusters, rank, columns), bf16), pltpu.VMEM((rows, columns), bf16), dma((parts,))],
        out_spec=HBM,
        flops=2 * rows * rank * columns, nbytes=6 * rows * columns,
    )


def solution(mesh):
    everywhere = ("top", "mid", "leaf")
    in_specs = (
        P(everywhere, None), P(everywhere, None), P(everywhere, None, None), P(everywhere, None, None),
        P(everywhere, None, None), P(everywhere, None, None), P(), P(everywhere, None, None, None),
        P(("top", "mid"), None, None, None), P("top", None, None, None), P(everywhere, None),
        P(("top", "mid"), None), P(("top", "mid"), None), P("top", None),
    )
    tops, mids, leaves = (mesh.shape[axis] for axis in everywhere)

    def run(*args):
        return body(*args, tops=tops, mids=mids, leaves=leaves)

    return jax.shard_map(
        run, mesh=mesh, in_specs=in_specs, out_specs=P(everywhere, None), check_vma=False
    )
```

```python
import functools

import jax
import jax.numpy as jnp
from jax import lax
from jax.experimental import pallas as pl
from jax.experimental.pallas import tpu as pltpu
from jax.sharding import PartitionSpec as P


damping = 0.7
f32 = jnp.float32
bf16 = jnp.bfloat16
VMEM = pl.BlockSpec(memory_space=pltpu.VMEM)


def mm(a, b):
    return jnp.dot(a, b, preferred_element_type=f32)


def mtm(a, b):
    return lax.dot_general(a, b, (((0,), (0,)), ((), ())), preferred_element_type=f32)


HBM = pl.BlockSpec(memory_space=pltpu.HBM)


def call(kernel, outs, args, specs, scratch=(), limit=16, flops=0, nbytes=0, out_spec=VMEM):
    return pl.pallas_call(
        kernel,
        out_shape=outs,
        in_specs=specs,
        out_specs=jax.tree.map(lambda _: out_spec, outs),
        scratch_shapes=list(scratch),
        compiler_params=pltpu.CompilerParams(vmem_limit_bytes=limit << 20),
        cost_estimate=pl.CostEstimate(flops=flops, bytes_accessed=nbytes, transcendentals=0),
    )(*args)


def shape(dims, kind):
    return jax.ShapeDtypeStruct(dims, kind)


def at_home(value):
    return pltpu.with_memory_space_constraint(value, pltpu.HBM)


def spans(rows, parts):
    if rows % (16 * parts):
        parts = 1
    return [pl.ds(k * (rows // parts), rows // parts) for k in range(parts)]


def power_of_two(n):
    return n & (n - 1) == 0


def exchange(value, axes, size, steps):
    result = []
    for step in steps:
        result.append(lax.ppermute(value, axes, [(i, i ^ step) for i in range(size)]))
    return result


def gather_leaf(value, size):
    if power_of_two(size) and size <= 8:
        return [value] + exchange(value, "leaf", size, range(1, size))
    everything = lax.all_gather(value, "leaf")
    here = lax.axis_index("leaf")
    everything = jnp.take(everything, here ^ jnp.arange(size), axis=0)
    return [everything[k] for k in range(size)]


def cluster_steps(tops, mids):
    return [q for q in range(tops * mids) if not q & mids]


def gather_clusters(value, tops, mids):
    steps = cluster_steps(tops, mids)[1:]
    stack = jnp.concatenate([value] + exchange(value, ("top", "mid"), tops * mids, steps))
    return [stack, lax.ppermute(stack, "top", [(i, i ^ 1) for i in range(tops)])]


def coef_kernel(parts, bases, guess, transfer, message, bases_on, guess_on, transfer_on, sems, sem):
    columns = guess.shape[1]
    cuts = spans(guess.shape[0], parts)
    copies = []
    small = pltpu.make_async_copy(transfer, transfer_on, sem)
    small.start()
    for k, cut in enumerate(cuts):
        first = pltpu.make_async_copy(bases.at[cut, :], bases_on.at[cut, :], sems.at[0, k])
        second = pltpu.make_async_copy(guess.at[cut, :], guess_on.at[cut, :], sems.at[1, k])
        first.start()
        second.start()
        copies.append((first, second))
    small.wait()
    message[:, columns:] = transfer_on[...].T
    total = None
    for cut, (first, second) in zip(cuts, copies):
        first.wait()
        second.wait()
        term = mtm(bases_on[cut, :], guess_on[cut, :])
        total = term if total is None else total + term
    message[:, :columns] = total.astype(bf16)


def near_kernel(
    parts, mids, guess, bases, transfer, precond, diag, rhs, coupling, cc, gc, mid_transfer, *refs
):
    (lists_at, owner_at, clists_at, glists_at, f0, r7, coef, gw, ordered, far) = refs[:10]
    (w1, f0b, lists, owner, clists, glists, sems) = refs[10:]
    sources = (lists_at, owner_at, clists_at, glists_at)
    targets = (lists, owner, clists, glists)
    copies = [
        pltpu.make_async_copy(source, target, sems.at[k])
        for k, (source, target) in enumerate(zip(sources, targets))
    ]
    for copy in copies:
        copy.start()
    cuts = spans(guess.shape[0], parts)
    ordered[...] = jnp.zeros_like(ordered)
    far[...] = jnp.zeros_like(far)
    flipped = bases[...].T
    for cut in cuts:
        r7[cut, :] = (damping * mm(precond[cut, :], bases[...])).astype(bf16)
    gmat = mm(flipped, r7[...]).astype(bf16)
    gw[0] = gmat
    gw[1] = mm(gmat, transfer[...]).astype(bf16)
    for cut in cuts:
        product = mm(diag[cut, :], guess[...])
        w1[cut, :] = (rhs[cut, :].astype(f32) - product).astype(bf16)
    for copy in copies:
        copy.wait()
    arrange(mids, lists, owner, clists, glists, coupling, cc, gc, mid_transfer, ordered, far)
    for cut in cuts:
        first = guess[cut, :].astype(f32) + damping * mm(precond[cut, :], w1[...])
        f0[cut, :] = first
        f0b[cut, :] = first.astype(bf16)
    coef[...] = mm(flipped, f0b[...])


def arrange(mids, lists, owner, clists, glists, coupling, cc, gc, mid_transfer, ordered, far):
    rank = cc.shape[1]
    size = ordered.shape[0]
    leaf = lax.axis_index("leaf")
    for k in range(coupling.shape[0]):
        slot = owner[0, lists[0, k]]
        at = slot ^ leaf if power_of_two(size) else slot
        ordered[at] = (ordered[at].astype(f32) + coupling[k].astype(f32)).astype(bf16)
    here = lax.axis_index("top") * mids + lax.axis_index("mid")

    def add(cluster, matrix):
        step = cluster ^ here
        core = lax.div(step, mids) & 1
        at = (step & (mids - 1)) + lax.div(step, 2 * mids) * mids
        columns = pl.ds(pl.multiple_of(at * rank, rank), rank)
        far[core, :, columns] = (far[core, :, columns].astype(f32) + matrix).astype(bf16)

    for k in range(cc.shape[0]):
        add(clists[0, k], cc[k].astype(f32))
    for k in range(gc.shape[0]):
        left = mm(mid_transfer[here], gc[k]).astype(bf16)
        for m in range(mids):
            at = glists[0, k] * mids + m
            both = lax.dot_general(
                left, mid_transfer[at], (((1,), (1,)), ((), ())), preferred_element_type=f32
            )
            add(at, both)


def leaf_kernel(size, ordered, coef, gw, *refs):
    messages = refs[:size]
    cluster, leaf_far, message = refs[size:]
    columns = coef.shape[1]
    total = None
    for k in range(size):
        up = mm(messages[k][:, columns:], messages[k][:, :columns]).astype(bf16).astype(f32)
        total = up if total is None else total + up
    cluster[...] = total.astype(bf16)
    far = None
    for k in range(size):
        term = mm(ordered[k], messages[k][:, :columns])
        far = term if far is None else far + term
    leaf_far[...] = far
    message[:, :columns] = (coef[...] - mm(gw[0], far.astype(bf16))).astype(bf16)
    message[:, columns:] = gw[1]


def fold_kernel(size, *refs):
    first, second = refs[:size], refs[size : 2 * size]
    base, hmat = refs[2 * size :]
    columns = base.shape[1]
    total = None
    for k in range(size):
        term = mm(first[k][:, columns:], second[k][...])
        total = term if total is None else total + term
    base[...] = total[:, :columns]
    hmat[...] = total[:, columns:].astype(bf16)


def cluster_total(far, packs):
    return (mm(far[0], packs[0][...]) + mm(far[1], packs[1][...])).astype(bf16)


def middle_kernel(far, base, hmat, mine, other, cluster, ctot):
    total = cluster_total(far, (mine, other))
    ctot[...] = total
    cluster[...] = (base[...] - mm(hmat[...], total)).astype(bf16)


def carry_kernel(parts, r7, transfer, out):
    for cut in spans(r7.shape[0], parts):
        out[cut, :] = mm(r7[cut, :], transfer[...]).astype(bf16)


def second_kernel(parts, done, rhs, diag, precond, r7, f0, lf1, ctot, transfer, out, w2, fb):
    cuts = spans(rhs.shape[0], parts)
    total = (lf1[...] + mm(transfer[...], ctot[...])).astype(bf16)
    for cut in cuts:
        first = f0[cut, :] - mm(r7[cut, :], total)
        out[cut, :] = first
        fb[cut, :] = first.astype(bf16)
    for cut in cuts:
        product = mm(diag[cut, :], fb[...])
        w2[cut, :] = (rhs[cut, :].astype(f32) - product).astype(bf16)
    for cut in cuts[:done]:
        out[cut, :] = out[cut, :] + damping * mm(precond[cut, :], w2[...])


def sibling_kernel(parts, done, size, ctot, ordered, near, precond, w2, r7, *refs):
    messages = refs[:size]
    out = refs[size]
    columns = ctot.shape[1]
    far = None
    for k in range(size):
        change = mm(messages[k][:, columns:], ctot[...])
        coefs = (messages[k][:, :columns].astype(f32) - change).astype(bf16)
        term = mm(ordered[k], coefs)
        far = term if far is None else far + term
    far = far.astype(bf16)
    for k, cut in enumerate(spans(near.shape[0], parts)):
        rest = near[cut, :] - mm(r7[cut, :], far)
        if k >= done:
            rest = rest + damping * mm(precond[cut, :], w2[...])
        out[cut, :] = rest


def last_kernel(parts, far, carried, near, mine, other, out, result, sems):
    total = cluster_total(far, (mine, other))
    copies = []
    for k, cut in enumerate(spans(near.shape[0], parts)):
        result[cut, :] = (near[cut, :] - mm(carried[cut, :], total)).astype(bf16)
        copy = pltpu.make_async_copy(result.at[cut, :], out.at[cut, :], sems.at[k])
        copy.start()
        copies.append(copy)
    for copy in copies:
        copy.wait()


def body(
    rhs, guess, diag_blocks, precond, bases, leaf_to_middle_transfer, mid_transfer,
    leaf_coupling, cluster_coupling, group_coupling, leaf_lists, owner, cluster_lists, group_lists,
    *, tops, mids, leaves,
):
    rows, columns = rhs.shape
    rank = bases.shape[2]
    diag, prec, basis = diag_blocks[0], precond[0], bases[0]
    transfer, coupling = leaf_to_middle_transfer[0], leaf_coupling[0]
    cc, gc = cluster_coupling[0], group_coupling[0]
    clusters = tops * mids
    parts, near_parts, done = 3, 3, 2
    dma = pltpu.SemaphoreType.DMA
    coef_bytes = rank * columns * 2

    message1, basis_on, guess_on, transfer_on = call(
        functools.partial(coef_kernel, parts),
        (shape((rank, columns + rank), bf16), shape((rows, rank), bf16), shape((rows, columns), bf16),
         shape((rank, rank), bf16)),
        [at_home(basis), at_home(guess), at_home(transfer)], [HBM] * 3, [dma((2, parts)), dma(())],
        flops=100000000000, nbytes=2 * rows * (rank + columns), limit=8,
    )
    messages1 = gather_leaf(message1, leaves)
    lists = (leaf_lists, owner, cluster_lists, group_lists)
    f0, r7, coef0, gw, ordered, far = call(
        functools.partial(near_kernel, near_parts, mids),
        (shape((rows, columns), f32), shape((rows, rank), bf16), shape((rank, columns), f32),
         shape((2, rank, rank), bf16), shape((leaves, rank, rank), bf16),
         shape((2, rank, clusters // 2 * rank), bf16)),
        [guess_on, basis_on, transfer_on, prec, diag, rhs, coupling, cc, gc, mid_transfer]
        + [at_home(value) for value in lists],
        [VMEM] * 10 + [HBM] * 4,
        [pltpu.VMEM((rows, columns), bf16)] * 2
        + [pltpu.SMEM(value.shape, jnp.int32) for value in lists] + [dma((len(lists),))],
        limit=24,
        flops=4 * rows * rows * (columns + rank // 2), nbytes=4 * rows * rows,
    )
    cluster1, lf1, message2 = call(
        functools.partial(leaf_kernel, leaves),
        (shape((rank, columns), bf16), shape((rank, columns), f32), shape((rank, columns + rank), bf16)),
        [ordered, coef0, gw, *messages1], [VMEM] * (3 + leaves),
        flops=2 * rank * rank * columns * (2 * leaves + 1), nbytes=2 * leaves * coef_bytes,
    )
    packs1 = gather_clusters(cluster1, tops, mids)
    messages2 = gather_leaf(message2, leaves)
    base, hmat = call(
        functools.partial(fold_kernel, leaves),
        (shape((rank, columns), f32), shape((rank, rank), bf16)),
        [*messages1, *messages2], [VMEM] * (2 * leaves),
        flops=2 * rank * rank * columns * 2 * leaves, nbytes=3 * leaves * coef_bytes,
    )
    cluster2, ctot = call(
        middle_kernel, (shape((rank, columns), bf16), shape((rank, columns), bf16)),
        [far, base, hmat, *packs1], [VMEM] * 5,
        flops=2 * rank * rank * columns * 10, nbytes=2 * clusters * coef_bytes,
    )
    packs2 = gather_clusters(cluster2, tops, mids)
    carried = call(
        functools.partial(carry_kernel, parts), shape((rows, rank), bf16),
        [r7, transfer_on], [VMEM] * 2,
        flops=2 * rows * rank * rank, nbytes=4 * rows * rank,
    )
    near, w2 = call(
        functools.partial(second_kernel, parts, done),
        (shape((rows, columns), f32), shape((rows, columns), bf16)),
        [rhs, diag, prec, r7, f0, lf1, ctot, transfer_on], [VMEM] * 8,
        [pltpu.VMEM((rows, columns), bf16)], limit=24,
        flops=4 * rows * rows * columns, nbytes=4 * rows * rows,
    )
    near = call(
        functools.partial(sibling_kernel, parts, done, leaves), shape((rows, columns), f32),
        [ctot, ordered, near, prec, w2, r7, *messages2], [VMEM] * (6 + leaves), limit=24,
        flops=2 * rows * rank * columns, nbytes=2 * leaves * coef_bytes,
    )
    return call(
        functools.partial(last_kernel, 2 * parts), shape((rows, columns), bf16),
        [far, carried, near, *packs2], [VMEM] * 5,
        [pltpu.VMEM((rows, columns), bf16), dma((2 * parts,))], out_spec=HBM,
        flops=2 * rows * rank * columns, nbytes=6 * rows * columns,
    )


def solution(mesh):
    everywhere = ("top", "mid", "leaf")
    in_specs = (
        P(everywhere, None), P(everywhere, None), P(everywhere, None, None), P(everywhere, None, None),
        P(everywhere, None, None), P(everywhere, None, None), P(), P(everywhere, None, None, None),
        P(("top", "mid"), None, None, None), P("top", None, None, None), P(everywhere, None),
        P(("top", "mid"), None), P(("top", "mid"), None), P("top", None),
    )
    tops, mids, leaves = (mesh.shape[axis] for axis in everywhere)

    def run(*args):
        return body(*args, tops=tops, mids=mids, leaves=leaves)

    return jax.shard_map(
        run, mesh=mesh, in_specs=in_specs, out_specs=P(everywhere, None), check_vma=False
    )
```
